32 devices in a mesh: dp: 8 (over z, y), mp: 4 (over x, core).
Axes of the slice: x: 2, y: 2, z: 4, core: 2. Of those that a mesh axis runs over, the one named last changes fastest.
Arguments:
- hidden: bfloat16 [8192, 5120], P('dp'), may hold values from -6 to 6
- exit_depth: int32 [8192], P('dp'), may hold values from 0 to 3, as said below
- seq_ids: int32 [8192], P('dp'), may hold values from 0 to 3, as said below
- dest: int32 [8192], P('dp'), may hold values from 0 to 7, as said below
- norm_gain: bfloat16 [5120], replicated, may hold values from 0.5 to 1.5
- w_query: bfloat16 [5120, 3072], P(None, 'mp'), may hold values from -4 to 4
- w_key: bfloat16 [5120, 3072], P(None, 'mp'), may hold values from -4 to 4
- w_value: bfloat16 [5120, 3072], P(None, 'mp'), may hold values from -0.078125 to 0.078125
- w_out: bfloat16 [3072, 5120], P('mp'), may hold values from -0.4375 to 0.4375
Outputs:
- next_rows: bfloat16 [6144, 5120], P('dp', 'mp')
The draws below stay inside these ranges and needn't reach their ends.
Inputs may be any that keep to these rules, and one draw needn't show every extreme that they name: exit_depth is 3 for at most 768 tokens of one sequence, and for exactly that many in some sequence. seq_ids never fall along a sequence. `dest`: within one sequence, at most 96 tokens with exit depth 3 name the same destination, and some sequence has exactly 96 that do.
All inputs are finite; a program needn't handle non-finite values.
Results may differ from the reference program's by a relative error of at most 0.014.
Values may be sent and summed in bfloat16 or wider, within the bound.
A program may use at most 128 MiB of HBM per device.

```python
import math
import jax
import jax.numpy as jnp
from jax import lax

D = 5120
HD = 128
HEADS = 24
TOK_DEV = 1024
HW = 3072
TOKENS = 8192
SLOTS = 768
CAP = 96
N_DP = 8
N_MP = 4


def routing_plan(key):
    base = jax.random.fold_in(key, 4242)
    key_level, key_forced, key_rows, key_buckets, key_spare, key_depth = jax.random.split(base, 6)
    level = jax.random.randint(key_level, (N_DP,), 1, 13)
    forced = jax.random.randint(key_forced, (), 0, N_DP)
    level = jnp.where(jnp.arange(N_DP) == forced, 12, level)
    counts = level * (TOK_DEV // 16)

    def row_order(sub_key):
        return jax.random.permutation(sub_key, TOK_DEV)

    def bucket_order(sub_key):
        return jax.random.permutation(sub_key, N_DP)
    ranks = jax.vmap(row_order)(jax.random.split(key_rows, N_DP))
    buckets = jax.vmap(bucket_order)(jax.random.split(key_buckets, N_DP))
    active = ranks < counts[:, None]
    bucket = jnp.minimum(ranks // CAP, N_DP - 1)
    live_dest = jnp.take_along_axis(buckets, bucket, axis=1)
    spare = jax.random.randint(key_spare, (N_DP, TOK_DEV), 0, N_DP)
    target = jnp.where(active, live_dest, spare)
    depth = jnp.where(active, 3, jax.random.randint(key_depth, (N_DP, TOK_DEV), 0, 3))
    return (depth.reshape(-1).astype(jnp.int32), target.reshape(-1).astype(jnp.int32))


def draw_exit_depth(key, part):
    return routing_plan(key)[0]


def draw_dest(key, part):
    return routing_plan(key)[1]


def draw_seq_ids(key, part):
    cut_key = jax.random.fold_in(key, 777)
    cuts = jax.random.randint(cut_key, (N_DP, 3), 1, TOK_DEV)
    places = jnp.arange(TOK_DEV)
    documents = jnp.sum((places[None, :, None] >= cuts[:, None, :]).astype(jnp.int32), axis=2)
    return documents.reshape(-1).astype(jnp.int32)


def projection_draw(key, salt):
    base_draw = jax.random.truncated_normal(jax.random.fold_in(key, salt), -6.0, 6.0, (D, HW), jnp.float32) / math.sqrt(D)
    return base_draw


def draw_w_query(key, part):
    return projection_draw(key, 31).astype(jnp.bfloat16)


def draw_w_key(key, part):
    return projection_draw(key, 32).astype(jnp.bfloat16)


def draw_hidden(key, part):
    noise_rows = jax.random.truncated_normal(jax.random.fold_in(key, 51), -6.0, 6.0, (N_DP, TOK_DEV, D), jnp.float32)
    return noise_rows.reshape(TOKENS, D).astype(jnp.bfloat16)


def block_levels(own_key, shape, pieces, smallest, high):
    factor_of, own = 1.0, jax.random.fold_in(own_key, 6)
    for dim, shards_of in pieces:
        steps = jnp.exp(jax.random.uniform(jax.random.fold_in(own, dim), (shards_of,), jnp.float32, smallest / len(pieces), high / len(pieces)))
        factor_of = factor_of * jnp.repeat(steps, shape[dim] // shards_of).reshape([-1 if axis == dim else 1 for axis in range(len(shape))])
    return factor_of


def noise(stream_key, shape, width, bound, pieces=(), held_as=jnp.bfloat16):
    values = width * jax.random.normal(stream_key, shape, jnp.float32)
    if pieces:
        values = values * block_levels(stream_key, shape, pieces, -0.22, 0.18)
    return jnp.clip(values, -bound, bound).astype(held_as)


def setup_inputs(seed: int = 0) -> dict:
    key_of = jax.random.split(jax.random.key(seed), 10)
    hidden = draw_hidden(jax.random.fold_in(key_of[9], 71), 0)
    exit_depth = draw_exit_depth(jax.random.fold_in(key_of[9], 71), 0)
    seq_ids = draw_seq_ids(jax.random.fold_in(key_of[9], 71), 0)
    dest = draw_dest(jax.random.fold_in(key_of[9], 71), 0)
    norm_gain = jnp.clip(1.0 + 0.1 * jax.random.normal(key_of[4], (D,), jnp.float32), 0.5, 1.5).astype(jnp.bfloat16)
    w_query = draw_w_query(jax.random.fold_in(key_of[9], 71), 0)
    w_key = draw_w_key(jax.random.fold_in(key_of[9], 71), 0)
    w_value = noise(key_of[7], (D, HW), D ** -0.5, 0.078125, ((1, 4),))
    w_out = noise(key_of[8], (HW, D), (HW // 16) ** -0.5, 0.4375, ((0, 4),))
    return {"hidden": hidden, "exit_depth": exit_depth, "seq_ids": seq_ids, "dest": dest, "norm_gain": norm_gain, "w_query": w_query, "w_key": w_key, "w_value": w_value, "w_out": w_out}


def rotate_pairs(values, places):
    half_width = values.shape[-1] // 2
    frequency = 10000.0 ** (-jnp.arange(half_width, dtype=jnp.float32) / half_width)
    angle = places[:, None] * frequency[None, :]
    cosine = jnp.cos(angle)[:, None, :]
    sine_term = jnp.sin(angle)[:, None, :]
    first = values[..., :half_width]
    second = values[..., half_width:]
    return jnp.concatenate([first * cosine - second * sine_term, second * cosine + first * sine_term], axis=-1)

def normalize(rows, norm_gain):
    widened = rows.astype(jnp.float32)
    mean_square = lax.optimization_barrier(jnp.mean(widened * widened, axis=-1, keepdims=True))
    return (widened * lax.rsqrt(mean_square + 1e-05) * norm_gain.astype(jnp.float32)).astype(jnp.bfloat16)

def reference(hidden, exit_depth, seq_ids, dest, norm_gain, w_query, w_key, w_value, w_out):
    scale_factor = 1.0 / math.sqrt(HD)
    places = jnp.arange(TOK_DEV, dtype=jnp.float32)
    group_width = HEADS * HD // N_MP
    out_groups = w_out.astype(jnp.float32).reshape(N_MP, group_width, D)

    def one_sequence(operands):
        rows, documents = operands
        normed = normalize(rows, norm_gain)

        def project(weight):
            return jnp.dot(normed, weight, preferred_element_type=jnp.float32).reshape(TOK_DEV, HEADS, HD)
        queries = rotate_pairs(project(w_query), places).astype(jnp.bfloat16)
        keys = rotate_pairs(project(w_key), places).astype(jnp.bfloat16)
        values = project(w_value).astype(jnp.bfloat16)
        scores = jnp.einsum('qhd,khd->hqk', queries.astype(jnp.float32), keys.astype(jnp.float32)) * scale_factor
        allowed = (documents[:, None] == documents[None, :]) & (places[None, :] <= places[:, None])
        scores = jnp.where(allowed[None], scores, -1e+30)
        highest = lax.optimization_barrier(jnp.max(scores, axis=-1, keepdims=True))
        raised = jnp.exp(scores - highest)
        probs = (raised / lax.optimization_barrier(jnp.sum(raised, axis=-1, keepdims=True))).astype(jnp.bfloat16)
        attended = jnp.einsum('hqk,khd->qhd', probs.astype(jnp.float32), values.astype(jnp.float32))
        attended = attended.astype(jnp.bfloat16).reshape(TOK_DEV, N_MP, group_width)
        partials = jnp.einsum('tgc,gcd->gtd', attended.astype(jnp.float32), out_groups)
        partials = lax.optimization_barrier(partials.astype(jnp.bfloat16)).astype(jnp.float32)
        return (rows.astype(jnp.float32) + lax.optimization_barrier(jnp.sum(partials, axis=0))).astype(jnp.bfloat16)
    updated = lax.map(one_sequence, (hidden.reshape(N_DP, TOK_DEV, D), seq_ids.reshape(N_DP, TOK_DEV)))
    active = (exit_depth == 3).reshape(N_DP, TOK_DEV)
    targets = dest.reshape(N_DP, TOK_DEV)
    chosen = ((targets[:, :, None] == jnp.arange(N_DP, dtype=jnp.int32)[None, None, :]) & active[:, :, None]).astype(jnp.int32)
    running = jnp.cumsum(chosen, axis=1)
    order_rank = lax.optimization_barrier(jnp.sum(running * chosen, axis=2)) - 1
    sources = jnp.arange(N_DP, dtype=jnp.int32)[:, None]
    slot_of = jnp.where(active, targets * SLOTS + sources * CAP + order_rank, N_DP * SLOTS).astype(jnp.int32)
    result = jnp.zeros((N_DP * SLOTS, D), jnp.bfloat16)
    return result.at[slot_of.reshape(-1)].set(updated.reshape(-1, D), mode='drop')
```

```python
import functools
import math

import jax
import jax.numpy as jnp
import numpy as np
from jax import lax
from jax.experimental import pallas as pl
from jax.experimental.pallas import tpu as pltpu
from jax.sharding import PartitionSpec as P

HD = 128
ANY = pl.ANY
VMEM = pltpu.VMEM


def rope_tables(tokens):
    half = HD // 2
    frequency = 10000.0 ** (-np.arange(half, dtype=np.float64) / half)
    angle = np.arange(tokens, dtype=np.float64)[:, None] * frequency[None, :]
    cosine, sine = np.cos(angle), np.sin(angle)
    return (
        np.concatenate([cosine, cosine], axis=1).astype(np.float32),
        np.concatenate([-sine, sine], axis=1).astype(np.float32),
    )


def qkv_kernel(
    blocks, bn, rows, hidden, gain, wq, wk, wv, cosine, sine, out, held, normed, wbuf, hsem, wsem
):
    step = pl.program_id(0)
    slot = lax.rem(step, 2)
    chunks = hidden.shape[0] // rows

    def fetch(index, do):
        for which, w in enumerate((wq, wk, wv)):

            @pl.when(index // blocks == which)
            def _():
                column = pl.multiple_of(lax.rem(index, blocks) * bn, bn)
                to = lax.rem(index, 2)
                do(pltpu.make_async_copy(w.at[:, pl.ds(column, bn)], wbuf.at[to], wsem.at[to]))

    def hidden_copy(r):
        part = pl.ds(r * rows, rows)
        return pltpu.make_async_copy(hidden.at[part], held.at[part], hsem.at[r])

    @pl.when(step == 0)
    def _():
        for r in range(chunks):
            hidden_copy(r).start()
        fetch(0, lambda c: c.start())

    @pl.when(step + 1 < 3 * blocks)
    def _():
        fetch(step + 1, lambda c: c.start())

    @pl.when(step == 0)
    def _():
        def normalize(r, carry):
            hidden_copy(r).wait()
            part = pl.ds(pl.multiple_of(r * rows, rows), rows)
            x = held[part, :].astype(jnp.float32)
            mean_square = jnp.mean(x * x, axis=-1, keepdims=True)
            y = x * lax.rsqrt(mean_square + 1e-05) * gain[...].astype(jnp.float32)
            normed[part, :] = y.astype(jnp.bfloat16)
            return carry

        lax.fori_loop(0, chunks, normalize, 0)

    fetch(step, lambda c: c.wait())
    big = 2 * rows

    def product(r, rotate):
        part = pl.ds(pl.multiple_of(r * big, big), big)
        y = jnp.dot(normed[part, :], wbuf[slot], preferred_element_type=jnp.float32)
        for h in range(bn // HD):
            lanes = slice(h * HD, (h + 1) * HD)
            z = y[:, lanes]
            if rotate:
                z = z * cosine[part, :] + pltpu.roll(z, HD // 2, 1) * sine[part, :]
            out[0, part, lanes] = z.astype(jnp.bfloat16)

    for rotate in (True, False):

        @pl.when((step < 2 * blocks) == rotate)
        def _():
            def go(r, carry):
                product(r, rotate)
                return carry

            lax.fori_loop(0, hidden.shape[0] // big, go, 0)


def project(hidden, gain, wq, wk, wv):
    tokens, width = hidden.shape
    hw = wq.shape[1]
    bn = 256 if hw % 256 == 0 else HD
    blocks = hw // bn
    rows = 128
    cosine, sine = rope_tables(tokens)
    whole = lambda *shape: pl.BlockSpec(shape, lambda i: (0,) * len(shape), pipeline_mode=pl.Buffered(1))
    return pl.pallas_call(
        functools.partial(qkv_kernel, blocks, bn, rows),
        grid=(3 * blocks,),
        out_shape=jax.ShapeDtypeStruct((3, tokens, hw), jnp.bfloat16),
        in_specs=[
            pl.BlockSpec(memory_space=ANY),
            whole(1, width),
            pl.BlockSpec(memory_space=ANY),
            pl.BlockSpec(memory_space=ANY),
            pl.BlockSpec(memory_space=ANY),
            whole(tokens, HD),
            whole(tokens, HD),
        ],
        out_specs=pl.BlockSpec((1, tokens, bn), lambda i: (i // blocks, 0, lax.rem(i, blocks))),
        scratch_shapes=[
            VMEM((tokens, width), jnp.bfloat16),
            VMEM((tokens, width), jnp.bfloat16),
            VMEM((2, width, bn), jnp.bfloat16),
            pltpu.SemaphoreType.DMA((tokens // rows,)),
            pltpu.SemaphoreType.DMA((2,)),
        ],
        compiler_params=pltpu.CompilerParams(vmem_limit_bytes=60 * 2**20),
        name="qkv",
    )(hidden, gain.reshape(1, width), wq, wk, wv, cosine, sine)


def attention_kernel(capacity, q, k, v, meta_row, meta_col, out, pick, bias, attended):
    tokens = q.shape[1]
    slots = out.shape[0]
    block = 256
    scale = 1.0 / math.sqrt(HD)

    @pl.when(pl.program_id(0) == 0)
    def _():
        code = meta_row[1:2, :]
        rank = jnp.zeros((1, tokens), jnp.float32)
        for b in range(tokens // block):
            part = slice(b * block, (b + 1) * block)
            below = lax.broadcasted_iota(jnp.int32, (block, tokens), 0) + b * block
            across = lax.broadcasted_iota(jnp.int32, (block, tokens), 1)
            earlier = (meta_col[part, 1:2] == code) & (below < across)
            rank += jnp.sum(jnp.where(earlier, 1.0, 0.0), axis=0, keepdims=True)
            allowed = (meta_col[part, 0:1] == meta_row[0:1, :]) & (across <= below)
            bias[part, :] = jnp.where(allowed, 0.0, -1e30)
        slot = jnp.where(code >= 0, code * capacity + rank.astype(jnp.int32), -1)
        for s in range(0, slots, 128):
            row = lax.broadcasted_iota(jnp.int32, (128, tokens), 0) + s
            pick[s : s + 128, :] = jnp.where(row == slot, 1.0, 0.0).astype(jnp.bfloat16)

    for b in range(tokens // block):
        part = slice(b * block, (b + 1) * block)
        end = (b + 1) * block
        scores = lax.dot_general(
            q[0, part, :], k[0, :end, :], (((1,), (1,)), ((), ())), preferred_element_type=jnp.float32
        )
        scores = scores * scale + bias[part, :end]
        raised = jnp.exp(scores - jnp.max(scores, axis=-1, keepdims=True))
        total = jnp.sum(raised, axis=-1, keepdims=True)
        mixed = jnp.dot(raised.astype(jnp.bfloat16), v[0, :end, :], preferred_element_type=jnp.float32)
        attended[part, :] = (mixed / total).astype(jnp.bfloat16)
    out[...] = jnp.dot(pick[...], attended[...], preferred_element_type=jnp.float32).astype(jnp.bfloat16)


def attend(qkv, meta, slots, capacity):
    _, tokens, hw = qkv.shape
    part = lambda which: pl.BlockSpec((1, tokens, HD), lambda h: (which, 0, h))
    return pl.pallas_call(
        functools.partial(attention_kernel, capacity),
        grid=(hw // HD,),
        out_shape=(
            jax.ShapeDtypeStruct((slots, hw), jnp.bfloat16),
            jax.ShapeDtypeStruct((slots, tokens), jnp.bfloat16),
        ),
        in_specs=[
            part(0),
            part(1),
            part(2),
            pl.BlockSpec((2, tokens), lambda h: (0, 0)),
            pl.BlockSpec((tokens, 2), lambda h: (0, 0)),
        ],
        out_specs=(
            pl.BlockSpec((slots, HD), lambda h: (0, h)),
            pl.BlockSpec((slots, tokens), lambda h: (0, 0)),
        ),
        scratch_shapes=[VMEM((tokens, tokens), jnp.float32), VMEM((tokens, HD), jnp.bfloat16)],
        compiler_params=pltpu.CompilerParams(vmem_limit_bytes=48 * 2**20),
        name="attend",
    )(qkv, qkv, qkv, meta, meta.T)


def body(hidden, exit_depth, seq_ids, dest, norm_gain, w_query, w_key, w_value, w_out):
    peers = lax.axis_size("dp")
    groups = lax.axis_size("mp")
    tokens, width = hidden.shape
    slots = 3 * tokens // 4
    capacity = slots // peers
    feature_slice = width // groups
    meta = jnp.stack([seq_ids, jnp.where(exit_depth == 3, dest, -1)])
    qkv = project(hidden, norm_gain, w_query, w_key, w_value)
    attended, pick = attend(qkv, meta, slots, capacity)
    own_hidden = lax.dynamic_slice_in_dim(
        hidden, lax.axis_index("mp") * feature_slice, feature_slice, 1
    )
    partial_value = jnp.dot(attended, w_out, preferred_element_type=jnp.float32).astype(jnp.bfloat16)
    own_features = jnp.dot(pick, own_hidden, preferred_element_type=jnp.float32)
    summed = lax.psum_scatter(partial_value, "mp", scatter_dimension=1, tiled=True).astype(
        jnp.float32
    )
    updated = (own_features + summed).astype(jnp.bfloat16)
    return lax.all_to_all(updated, "dp", split_axis=0, concat_axis=0, tiled=True)


def solution(mesh):
    return jax.shard_map(
        body,
        mesh=mesh,
        in_specs=(
            P("dp", None),
            P("dp"),
            P("dp"),
            P("dp"),
            P(),
            P(None, "mp"),
            P(None, "mp"),
            P(None, "mp"),
            P("mp", None),
        ),
        out_specs=P("dp", "mp"),
        check_vma=False,
    )
```

```python
import functools
import math

import jax
import jax.numpy as jnp
import numpy as np
from jax import lax
from jax.experimental import pallas as pl
from jax.experimental.pallas import tpu as pltpu
from jax.sharding import PartitionSpec as P

HD = 128
CHUNK = 256
ANY = pl.ANY
VMEM = pltpu.VMEM


def rope_tables(tokens):
    half = HD // 2
    frequency = 10000.0 ** (-np.arange(half, dtype=np.float64) / half)
    angle = np.arange(tokens, dtype=np.float64)[:, None] * frequency[None, :]
    cosine, sine = np.cos(angle), np.sin(angle)
    return (
        np.concatenate([cosine, cosine], axis=1).astype(np.float32),
        np.concatenate([-sine, sine], axis=1).astype(np.float32),
    )


def qkv_kernel(
    blocks, bn, rows, hidden, gain, wq, wk, wv, cosine, sine, out, held, normed, wbuf, hsem, wsem
):
    step = pl.program_id(0)
    slot = lax.rem(step, 2)
    chunks = hidden.shape[0] // rows

    def fetch(index, do):
        for which, w in enumerate((wq, wk, wv)):

            @pl.when(index // blocks == which)
            def _():
                column = pl.multiple_of(lax.rem(index, blocks) * bn, bn)
                to = lax.rem(index, 2)
                do(pltpu.make_async_copy(w.at[:, pl.ds(column, bn)], wbuf.at[to], wsem.at[to]))

    def hidden_copy(r):
        part = pl.ds(r * rows, rows)
        return pltpu.make_async_copy(hidden.at[part], held.at[part], hsem.at[r])

    @pl.when(step == 0)
    def _():
        for r in range(chunks):
            hidden_copy(r).start()
        fetch(0, lambda c: c.start())

    @pl.when(step + 1 < 3 * blocks)
    def _():
        fetch(step + 1, lambda c: c.start())

    @pl.when(step == 0)
    def _():
        def normalize(r, carry):
            hidden_copy(r).wait()
            part = pl.ds(pl.multiple_of(r * rows, rows), rows)
            x = held[part, :].astype(jnp.float32)
            mean_square = jnp.mean(x * x, axis=-1, keepdims=True)
            y = x * lax.rsqrt(mean_square + 1e-05) * gain[...].astype(jnp.float32)
            normed[part, :] = y.astype(jnp.bfloat16)
            return carry

        lax.fori_loop(0, chunks, normalize, 0)

    fetch(step, lambda c: c.wait())
    big = 2 * rows

    def product(r, rotate):
        part = pl.ds(pl.multiple_of(r * big, big), big)
        y = jnp.dot(normed[part, :], wbuf[slot], preferred_element_type=jnp.float32)
        for h in range(bn // HD):
            lanes = slice(h * HD, (h + 1) * HD)
            z = y[:, lanes]
            if rotate:
                z = z * cosine[part, :] + pltpu.roll(z, HD // 2, 1) * sine[part, :]
            out[0, part, lanes] = z.astype(jnp.bfloat16)

    for rotate in (True, False):

        @pl.when((step < 2 * blocks) == rotate)
        def _():
            def go(r, carry):
                product(r, rotate)
                return carry

            lax.fori_loop(0, hidden.shape[0] // big, go, 0)


def project(hidden, gain, wq, wk, wv):
    tokens, width = hidden.shape
    hw = wq.shape[1]
    bn = 256 if hw % 256 == 0 else HD
    blocks = hw // bn
    rows = 128
    cosine, sine = rope_tables(tokens)
    whole = lambda *shape: pl.BlockSpec(shape, lambda i: (0,) * len(shape), pipeline_mode=pl.Buffered(1))
    return pl.pallas_call(
        functools.partial(qkv_kernel, blocks, bn, rows),
        grid=(3 * blocks,),
        out_shape=jax.ShapeDtypeStruct((3, tokens, hw), jnp.bfloat16),
        in_specs=[
            pl.BlockSpec(memory_space=ANY),
            whole(1, width),
            pl.BlockSpec(memory_space=ANY),
            pl.BlockSpec(memory_space=ANY),
            pl.BlockSpec(memory_space=ANY),
            whole(tokens, HD),
            whole(tokens, HD),
        ],
        out_specs=pl.BlockSpec((1, tokens, bn), lambda i: (i // blocks, 0, lax.rem(i, blocks))),
        scratch_shapes=[
            VMEM((tokens, width), jnp.bfloat16),
            VMEM((tokens, width), jnp.bfloat16),
            VMEM((2, width, bn), jnp.bfloat16),
            pltpu.SemaphoreType.DMA((tokens // rows,)),
            pltpu.SemaphoreType.DMA((2,)),
        ],
        compiler_params=pltpu.CompilerParams(vmem_limit_bytes=60 * 2**20),
        name="qkv",
    )(hidden, gain.reshape(1, width), wq, wk, wv, cosine, sine)


def attention_kernel(capacity, q, k, v, meta_row, meta_col, out, pick, bias, attended):
    tokens = q.shape[1]
    slots = out.shape[0]
    block = 256
    scale = 1.0 / math.sqrt(HD)

    @pl.when(pl.program_id(0) == 0)
    def _():
        code = meta_row[1:2, :]
        rank = jnp.zeros((1, tokens), jnp.float32)
        for b in range(tokens // block):
            part = slice(b * block, (b + 1) * block)
            below = lax.broadcasted_iota(jnp.int32, (block, tokens), 0) + b * block
            across = lax.broadcasted_iota(jnp.int32, (block, tokens), 1)
            earlier = (meta_col[part, 1:2] == code) & (below < across)
            rank += jnp.sum(jnp.where(earlier, 1.0, 0.0), axis=0, keepdims=True)
            allowed = (meta_col[part, 0:1] == meta_row[0:1, :]) & (across <= below)
            bias[part, :] = jnp.where(allowed, 0.0, -1e30)
        slot = jnp.where(code >= 0, code * capacity + rank.astype(jnp.int32), -1)
        for s in range(0, slots, 128):
            row = lax.broadcasted_iota(jnp.int32, (128, tokens), 0) + s
            pick[s : s + 128, :] = jnp.where(row == slot, 1.0, 0.0).astype(jnp.bfloat16)

    for b in range(tokens // block):
        part = slice(b * block, (b + 1) * block)
        end = (b + 1) * block
        scores = lax.dot_general(
            q[0, part, :], k[0, :end, :], (((1,), (1,)), ((), ())), preferred_element_type=jnp.float32
        )
        scores = scores * scale + bias[part, :end]
        raised = jnp.exp(scores - jnp.max(scores, axis=-1, keepdims=True))
        total = jnp.sum(raised, axis=-1, keepdims=True)
        mixed = jnp.dot(raised.astype(jnp.bfloat16), v[0, :end, :], preferred_element_type=jnp.float32)
        attended[part, :] = (mixed / total).astype(jnp.bfloat16)
    out[...] = jnp.dot(pick[...], attended[...], preferred_element_type=jnp.float32).astype(jnp.bfloat16)


def attend(qkv, meta, slots, capacity):
    _, tokens, hw = qkv.shape
    part = lambda which: pl.BlockSpec((1, tokens, HD), lambda h: (which, 0, h))
    return pl.pallas_call(
        functools.partial(attention_kernel, capacity),
        grid=(hw // HD,),
        out_shape=(
            jax.ShapeDtypeStruct((slots, hw), jnp.bfloat16),
            jax.ShapeDtypeStruct((slots, tokens), jnp.bfloat16),
        ),
        in_specs=[
            part(0),
            part(1),
            part(2),
            pl.BlockSpec((2, tokens), lambda h: (0, 0)),
            pl.BlockSpec((tokens, 2), lambda h: (0, 0)),
        ],
        out_specs=(
            pl.BlockSpec((slots, HD), lambda h: (0, h)),
            pl.BlockSpec((slots, tokens), lambda h: (0, 0)),
        ),
        scratch_shapes=[VMEM((tokens, tokens), jnp.float32), VMEM((tokens, HD), jnp.bfloat16)],
        compiler_params=pltpu.CompilerParams(vmem_limit_bytes=48 * 2**20),
        name="attend",
    )(qkv, qkv, qkv, meta, meta.T)


def out_kernel(
    peers, groups, att, pick, hidden, w_out, out,
    wbuf, residual, pair_send, pair_own, pair_recv, x_send, x_recv, acc, updated,
    wsem, rsem, pair_ssem, pair_rsem, x_ssem, x_rsem, row_ssem, row_rsem, own_sem,
):
    chunks, _, slots, cw = pair_send.shape
    capacity = slots // peers
    inner = w_out.shape[0]
    feature_slice = w_out.shape[1] // groups
    ring = groups // 2
    d, m = lax.axis_index("dp"), lax.axis_index("mp")
    core, x = lax.rem(m, 2), m // 2
    partner = x * 2 + 1 - core

    def x_to(r):
        return lax.rem(x + r, ring)

    def lane(n, j):
        return pl.ds(pl.multiple_of(n * feature_slice + j * cw, HD), cw)

    def weight_copy(j, n):
        return pltpu.make_async_copy(w_out.at[:, lane(n, j)], wbuf.at[j, n], wsem.at[j, n])

    def residual_copy(j):
        return pltpu.make_async_copy(hidden.at[:, lane(m, j)], residual.at[j], rsem.at[j])

    def pair_copy(j):
        return pltpu.make_async_remote_copy(
            src_ref=pair_send.at[j], dst_ref=pair_recv.at[j],
            send_sem=pair_ssem.at[j], recv_sem=pair_rsem.at[j],
            device_id={"mp": partner}, device_id_type=pl.DeviceIdType.MESH,
        )

    def x_copy(j, r):
        return pltpu.make_async_remote_copy(
            src_ref=x_send.at[j, r - 1], dst_ref=x_recv.at[j, r - 1],
            send_sem=x_ssem.at[j, r - 1], recv_sem=x_rsem.at[j, r - 1],
            device_id={"mp": x_to(r) * 2 + core}, device_id_type=pl.DeviceIdType.MESH,
        )

    def rows_of(t):
        return pl.ds(pl.multiple_of(t * capacity, 16), capacity)

    def own_rows(j):
        return out.at[rows_of(d), pl.ds(pl.multiple_of(j * cw, HD), cw)]

    def row_copy(j, i):
        to = lax.rem(d + i, peers)
        return pltpu.make_async_remote_copy(
            src_ref=updated.at[j, rows_of(to)], dst_ref=own_rows(j),
            send_sem=row_ssem.at[j, i], recv_sem=row_rsem.at[j, i],
            device_id={"dp": to}, device_id_type=pl.DeviceIdType.MESH,
        )

    def own_copy(j):
        return pltpu.make_async_copy(updated.at[j, rows_of(d)], own_rows(j), own_sem.at[j])

    for j in range(chunks):
        for n in range(groups):
            weight_copy(j, n).start()
        residual_copy(j).start()

    barrier = pltpu.get_barrier_semaphore()
    for i in range(1, peers):
        pl.semaphore_signal(
            barrier, inc=1, device_id={"dp": lax.rem(d + i, peers)}, device_id_type=pl.DeviceIdType.MESH
        )
    for r in range(1, ring):
        pl.semaphore_signal(
            barrier, inc=1, device_id={"mp": x_to(r) * 2 + core}, device_id_type=pl.DeviceIdType.MESH
        )
    pl.semaphore_signal(
        barrier, inc=1, device_id={"mp": partner}, device_id_type=pl.DeviceIdType.MESH
    )
    pl.semaphore_wait(barrier, peers + ring - 1)

    def multiply(j, n):
        return jnp.dot(att[...], wbuf[j, n], preferred_element_type=jnp.float32).astype(jnp.bfloat16)

    def step(s, carry):
        @pl.when(s < chunks)
        def _():
            for n in range(groups):
                weight_copy(s, n).wait()
            for r in range(ring):
                pair_send[s, r] = multiply(s, x_to(r) * 2 + 1 - core)
            pair_copy(s).start()
            for r in range(ring):
                pair_own[s, r] = multiply(s, x_to(r) * 2 + core)

        @pl.when((s >= 1) & (s <= chunks))
        def _():
            j = s - 1
            pair_copy(j).wait_recv()
            for r in range(1, ring):
                total = pair_own[j, r].astype(jnp.float32) + pair_recv[j, r].astype(jnp.float32)
                x_send[j, r - 1] = total.astype(jnp.bfloat16)
                x_copy(j, r).start()
            residual_copy(j).wait()
            kept = jnp.dot(pick[...], residual[j], preferred_element_type=jnp.float32)
            acc[j] = (
                kept + pair_own[j, 0].astype(jnp.float32) + pair_recv[j, 0].astype(jnp.float32)
            )

        @pl.when(s >= 2)
        def _():
            j = s - 2
            total = acc[j]
            for r in range(1, ring):
                x_copy(j, r).wait_recv()
                total += x_recv[j, r - 1].astype(jnp.float32)
            updated[j] = total.astype(jnp.bfloat16)
            for i in range(1, peers):
                row_copy(j, i).start()
            own_copy(j).start()

        return carry

    lax.fori_loop(0, chunks + 2, step, 0)

    def drain(j, carry):
        pair_copy(j).wait_send()
        for r in range(1, ring):
            x_copy(j, r).wait_send()
        own_copy(j).wait()
        for i in range(1, peers):
            row_copy(j, i).wait()
        return carry

    lax.fori_loop(0, chunks, drain, 0)


def finish(attended, pick, hidden, w_out, peers, groups):
    slots, inner = attended.shape
    tokens, width = hidden.shape
    feature_slice = width // groups
    cw = CHUNK if feature_slice % CHUNK == 0 else HD
    chunks = feature_slice // cw
    ring = groups // 2
    dma = pltpu.SemaphoreType.DMA
    bf16 = jnp.bfloat16
    vmem = pl.BlockSpec(memory_space=VMEM)
    far = pl.BlockSpec(memory_space=ANY)
    return pl.pallas_call(
        functools.partial(out_kernel, peers, groups),
        out_shape=jax.ShapeDtypeStruct((slots, feature_slice), bf16),
        in_specs=[vmem, vmem, far, far],
        out_specs=far,
        scratch_shapes=[
            VMEM((chunks, groups, inner, cw), bf16),
            VMEM((chunks, tokens, cw), bf16),
            VMEM((chunks, ring, slots, cw), bf16),
            VMEM((chunks, ring, slots, cw), bf16),
            VMEM((chunks, ring, slots, cw), bf16),
            VMEM((chunks, ring - 1, slots, cw), bf16),
            VMEM((chunks, ring - 1, slots, cw), bf16),
            VMEM((chunks, slots, cw), jnp.float32),
            VMEM((chunks, slots, cw), bf16),
            dma((chunks, groups)),
            dma((chunks,)),
            dma((chunks,)),
            dma((chunks,)),
            dma((chunks, ring - 1)),
            dma((chunks, ring - 1)),
            dma((chunks, peers)),
            dma((chunks, peers)),
            dma((chunks,)),
        ],
        compiler_params=pltpu.CompilerParams(
            collective_id=0, has_side_effects=True, vmem_limit_bytes=60 * 2**20
        ),
        name="finish",
    )(attended, pick, hidden, w_out)


def body(hidden, exit_depth, seq_ids, dest, norm_gain, w_query, w_key, w_value, w_out):
    peers = lax.axis_size("dp")
    groups = lax.axis_size("mp")
    tokens = hidden.shape[0]
    slots = 3 * tokens // 4
    capacity = slots // peers
    meta = jnp.stack([seq_ids, jnp.where(exit_depth == 3, dest, -1)])
    qkv = project(hidden, norm_gain, w_query, w_key, w_value)
    attended, pick = attend(qkv, meta, slots, capacity)
    return finish(attended, pick, hidden, w_out, peers, groups)


def solution(mesh):
    return jax.shard_map(
        body,
        mesh=mesh,
        in_specs=(
            P("dp", None),
            P("dp"),
            P("dp"),
            P("dp"),
            P(),
            P(None, "mp"),
            P(None, "mp"),
            P(None, "mp"),
            P("mp", None),
        ),
        out_specs=P("dp", "mp"),
        check_vma=False,
    )
```

```python
import functools
import math

import jax
import jax.numpy as jnp
import numpy as np
from jax import lax
from jax.experimental import pallas as pl
from jax.experimental.pallas import tpu as pltpu
from jax.sharding import PartitionSpec as P

HD = 128
CHUNKS = 8
LAG = 1
ANY = pl.ANY
VMEM = pltpu.VMEM


def rope_tables(tokens):
    half = HD // 2
    frequency = 10000.0 ** (-np.arange(half, dtype=np.float64) / half)
    angle = np.arange(tokens, dtype=np.float64)[:, None] * frequency[None, :]
    cosine, sine = np.cos(angle), np.sin(angle)
    return (
        np.concatenate([cosine, cosine], axis=1).astype(np.float32),
        np.concatenate([-sine, sine], axis=1).astype(np.float32),
    )


def qkv_kernel(
    blocks, bn, rows, hidden, gain, wq, wk, wv, cosine, sine, out, held, normed, wbuf, hsem, wsem
):
    step = pl.program_id(0)
    slot = lax.rem(step, 2)
    chunks = hidden.shape[0] // rows

    def fetch(index, do):
        for which, w in enumerate((wq, wk, wv)):

            @pl.when(index // blocks == which)
            def _():
                column = pl.multiple_of(lax.rem(index, blocks) * bn, bn)
                to = lax.rem(index, 2)
                do(pltpu.make_async_copy(w.at[:, pl.ds(column, bn)], wbuf.at[to], wsem.at[to]))

    def hidden_copy(r):
        part = pl.ds(r * rows, rows)
        return pltpu.make_async_copy(hidden.at[part], held.at[part], hsem.at[r])

    @pl.when(step == 0)
    def _():
        for r in range(chunks):
            hidden_copy(r).start()
        fetch(0, lambda c: c.start())

    @pl.when(step + 1 < 3 * blocks)
    def _():
        fetch(step + 1, lambda c: c.start())

    @pl.when(step == 0)
    def _():
        def normalize(r, carry):
            hidden_copy(r).wait()
            part = pl.ds(pl.multiple_of(r * rows, rows), rows)
            x = held[part, :].astype(jnp.float32)
            mean_square = jnp.mean(x * x, axis=-1, keepdims=True)
            y = x * lax.rsqrt(mean_square + 1e-05) * gain[...].astype(jnp.float32)
            normed[part, :] = y.astype(jnp.bfloat16)
            return carry

        lax.fori_loop(0, chunks, normalize, 0)

    fetch(step, lambda c: c.wait())
    big = 2 * rows

    def product(r, rotate):
        part = pl.ds(pl.multiple_of(r * big, big), big)
        y = jnp.dot(normed[part, :], wbuf[slot], preferred_element_type=jnp.float32)
        for h in range(bn // HD):
            lanes = slice(h * HD, (h + 1) * HD)
            z = y[:, lanes]
            if rotate:
                z = z * cosine[part, :] + pltpu.roll(z, HD // 2, 1) * sine[part, :]
            out[0, part, lanes] = z.astype(jnp.bfloat16)

    for rotate in (True, False):

        @pl.when((step < 2 * blocks) == rotate)
        def _():
            def go(r, carry):
                product(r, rotate)
                return carry

            lax.fori_loop(0, hidden.shape[0] // big, go, 0)


def project(hidden, gain, wq, wk, wv):
    tokens, width = hidden.shape
    hw = wq.shape[1]
    bn = 256 if hw % 256 == 0 else HD
    blocks = hw // bn
    rows = 128
    cosine, sine = rope_tables(tokens)
    whole = lambda *shape: pl.BlockSpec(shape, lambda i: (0,) * len(shape), pipeline_mode=pl.Buffered(1))
    return pl.pallas_call(
        functools.partial(qkv_kernel, blocks, bn, rows),
        grid=(3 * blocks,),
        out_shape=jax.ShapeDtypeStruct((3, tokens, hw), jnp.bfloat16),
        in_specs=[
            pl.BlockSpec(memory_space=ANY),
            whole(1, width),
            pl.BlockSpec(memory_space=ANY),
            pl.BlockSpec(memory_space=ANY),
            pl.BlockSpec(memory_space=ANY),
            whole(tokens, HD),
            whole(tokens, HD),
        ],
        out_specs=pl.BlockSpec((1, tokens, bn), lambda i: (i // blocks, 0, lax.rem(i, blocks))),
        scratch_shapes=[
            VMEM((tokens, width), jnp.bfloat16),
            VMEM((tokens, width), jnp.bfloat16),
            VMEM((2, width, bn), jnp.bfloat16),
            pltpu.SemaphoreType.DMA((tokens // rows,)),
            pltpu.SemaphoreType.DMA((2,)),
        ],
        compiler_params=pltpu.CompilerParams(vmem_limit_bytes=60 * 2**20),
        name="qkv",
    )(hidden, gain.reshape(1, width), wq, wk, wv, cosine, sine)


def tail_kernel(
    peers, groups, per_chunk, qkv, meta_row, meta_col, hidden, w_out, out,
    wbuf, residual, slot_row, pair_send, pair_own, pair_recv, x_send, x_recv, acc, updated,
    wsem, rsem, pair_ssem, pair_rsem, x_ssem, x_rsem, row_ssem, row_rsem, own_sem,
):
    chunks, ring, rows, feature_slice = pair_send.shape
    capacity = rows // per_chunk
    _, tokens, inner = qkv.shape
    d, m = lax.axis_index("dp"), lax.axis_index("mp")
    core, x = lax.rem(m, 2), m // 2
    partner = x * 2 + 1 - core
    scale = 1.0 / math.sqrt(HD)
    mesh_id = pl.DeviceIdType.MESH

    def x_to(r):
        return lax.rem(x + r, ring)

    def target(i):
        away = peers // 2 + ((i + 1) // 2) * (1 - 2 * lax.rem(i, 2))
        return lax.rem(d + away, peers)

    def weight_copy(n):
        columns = pl.ds(n * feature_slice, feature_slice)
        return pltpu.make_async_copy(w_out.at[:, columns], wbuf.at[n], wsem.at[n])

    def residual_copy():
        columns = pl.ds(pl.multiple_of(m * feature_slice, HD), feature_slice)
        return pltpu.make_async_copy(hidden.at[:, columns], residual, rsem)

    def pair_copy(j):
        return pltpu.make_async_remote_copy(
            src_ref=pair_send.at[j], dst_ref=pair_recv.at[j],
            send_sem=pair_ssem.at[j], recv_sem=pair_rsem.at[j],
            device_id={"mp": partner}, device_id_type=mesh_id,
        )

    def x_copy(j, r):
        return pltpu.make_async_remote_copy(
            src_ref=x_send.at[j, r - 1], dst_ref=x_recv.at[j, r - 1],
            send_sem=x_ssem.at[j, r - 1], recv_sem=x_rsem.at[j, r - 1],
            device_id={"mp": x_to(r) * 2 + core}, device_id_type=mesh_id,
        )

    def own_rows():
        return out.at[pl.ds(pl.multiple_of(d * capacity, 16), capacity)]

    def row_copy(j, k):
        return pltpu.make_async_remote_copy(
            src_ref=updated.at[j, pl.ds(k * capacity, capacity)], dst_ref=own_rows(),
            send_sem=row_ssem.at[j, k], recv_sem=row_rsem.at[j, k],
            device_id={"dp": target(j * per_chunk + k)}, device_id_type=mesh_id,
        )

    def own_copy():
        return pltpu.make_async_copy(
            updated.at[chunks - 1, pl.ds(rows - capacity, capacity)], own_rows(), own_sem
        )

    for n in range(groups):
        weight_copy(n).start()
    residual_copy().start()

    barrier = pltpu.get_barrier_semaphore()
    for i in range(1, peers):
        pl.semaphore_signal(
            barrier, inc=1, device_id={"dp": lax.rem(d + i, peers)}, device_id_type=mesh_id
        )
    for r in range(1, ring):
        pl.semaphore_signal(
            barrier, inc=1, device_id={"mp": x_to(r) * 2 + core}, device_id_type=mesh_id
        )
    pl.semaphore_signal(barrier, inc=1, device_id={"mp": partner}, device_id_type=mesh_id)

    code = meta_row[1:2, :]
    block = 256
    rank = jnp.zeros((1, tokens), jnp.float32)
    for b in range(tokens // block):
        below = lax.broadcasted_iota(jnp.int32, (block, tokens), 0) + b * block
        across = lax.broadcasted_iota(jnp.int32, (block, tokens), 1)
        earlier = (meta_col[b * block : (b + 1) * block, 1:2] == code) & (below < across)
        rank += jnp.sum(jnp.where(earlier, 1.0, 0.0), axis=0, keepdims=True)
    slot_row[...] = jnp.where(code >= 0, code * capacity + rank.astype(jnp.int32), -1)

    pl.semaphore_wait(barrier, peers + ring - 1)
    for n in range(groups):
        weight_copy(n).wait()
    residual_copy().wait()

    def chosen(j):
        parts = []
        for k in range(per_chunk):
            row = lax.broadcasted_iota(jnp.int32, (capacity, tokens), 0)
            parts.append((row + target(j * per_chunk + k) * capacity) == slot_row[...])
        return jnp.concatenate(parts, axis=0) if per_chunk > 1 else parts[0]

    def as_pick(hit):
        return jnp.where(hit, 1.0, 0.0).astype(jnp.bfloat16)

    def attend(j):
        hit = chosen(j)
        places = lax.broadcasted_iota(jnp.int32, (rows, tokens), 1)
        weight = jnp.where(hit, 1.0, 0.0)
        filled = jnp.sum(weight, axis=-1, keepdims=True)
        place = jnp.sum(jnp.where(hit, places, 0).astype(jnp.float32), axis=-1, keepdims=True)
        documents = meta_row[0:1, :].astype(jnp.float32)
        document = jnp.sum(jnp.where(hit, documents, 0.0), axis=-1, keepdims=True)
        allowed = (document == documents) & (places.astype(jnp.float32) <= place)
        bias = jnp.where(allowed, 0.0, -1e30)
        queries = jnp.dot(
            weight.astype(jnp.bfloat16), qkv[0], preferred_element_type=jnp.float32
        ).astype(jnp.bfloat16)
        heads = []
        for h in range(inner // HD):
            lanes = slice(h * HD, (h + 1) * HD)
            scores = lax.dot_general(
                queries[:, lanes], qkv[1, :, lanes], (((1,), (1,)), ((), ())),
                preferred_element_type=jnp.float32,
            )
            scores = scores * scale + bias
            raised = jnp.exp(scores - jnp.max(scores, axis=-1, keepdims=True))
            total = jnp.sum(raised, axis=-1, keepdims=True)
            mixed = jnp.dot(
                raised.astype(jnp.bfloat16), qkv[2, :, lanes], preferred_element_type=jnp.float32
            )
            heads.append((mixed * (filled / total)).astype(jnp.bfloat16))
        return jnp.concatenate(heads, axis=1)

    def multiply(attended, n):
        return jnp.dot(attended, wbuf[n], preferred_element_type=jnp.float32).astype(jnp.bfloat16)

    def step(s, carry):
        @pl.when(s < chunks)
        def _():
            attended = attend(s)
            for r in range(ring):
                pair_send[s, r] = multiply(attended, x_to(r) * 2 + 1 - core)
            pair_copy(s).start()
            for r in range(ring):
                pair_own[s, r] = multiply(attended, x_to(r) * 2 + core)
            pair_copy(s).wait_recv()
            for r in range(1, ring):
                total = pair_own[s, r].astype(jnp.float32) + pair_recv[s, r].astype(jnp.float32)
                x_send[s, r - 1] = total.astype(jnp.bfloat16)
                x_copy(s, r).start()
            kept = jnp.dot(as_pick(chosen(s)), residual[...], preferred_element_type=jnp.float32)
            acc[s] = (
                kept + pair_own[s, 0].astype(jnp.float32) + pair_recv[s, 0].astype(jnp.float32)
            )

        @pl.when(s >= LAG)
        def _():
            j = s - LAG
            total = acc[j]
            for r in range(1, ring):
                x_copy(j, r).wait_recv()
                total += x_recv[j, r - 1].astype(jnp.float32)
            updated[j] = total.astype(jnp.bfloat16)
            for k in range(per_chunk - 1):
                row_copy(j, k).start()

            @pl.when(j < chunks - 1)
            def _():
                row_copy(j, per_chunk - 1).start()

        return carry

    lax.fori_loop(0, chunks + LAG, step, 0)
    own_copy().start()

    def drain(j, carry):
        pair_copy(j).wait_send()
        for r in range(1, ring):
            x_copy(j, r).wait_send()
        for k in range(per_chunk - 1):
            row_copy(j, k).wait()

        @pl.when(j < chunks - 1)
        def _():
            row_copy(j, per_chunk - 1).wait()

        return carry

    lax.fori_loop(0, chunks, drain, 0)
    own_copy().wait()


def finish(qkv, meta, hidden, w_out, peers, groups):
    _, tokens, inner = qkv.shape
    slots = 3 * tokens // 4
    feature_slice = w_out.shape[1] // groups
    chunks = min(CHUNKS, peers)
    rows = slots // chunks
    ring = groups // 2
    dma = pltpu.SemaphoreType.DMA
    bf16 = jnp.bfloat16
    vmem = pl.BlockSpec(memory_space=VMEM)
    far = pl.BlockSpec(memory_space=ANY)
    per_chunk = peers // chunks
    return pl.pallas_call(
        functools.partial(tail_kernel, peers, groups, per_chunk),
        out_shape=jax.ShapeDtypeStruct((slots, feature_slice), bf16),
        in_specs=[vmem, vmem, vmem, far, far],
        out_specs=far,
        scratch_shapes=[
            VMEM((groups, inner, feature_slice), bf16),
            VMEM((tokens, feature_slice), bf16),
            VMEM((1, tokens), jnp.int32),
            VMEM((chunks, ring, rows, feature_slice), bf16),
            VMEM((chunks, ring, rows, feature_slice), bf16),
            VMEM((chunks, ring, rows, feature_slice), bf16),
            VMEM((chunks, ring - 1, rows, feature_slice), bf16),
            VMEM((chunks, ring - 1, rows, feature_slice), bf16),
            VMEM((chunks, rows, feature_slice), jnp.float32),
            VMEM((chunks, rows, feature_slice), bf16),
            dma((groups,)),
            dma,
            dma((chunks,)),
            dma((chunks,)),
            dma((chunks, ring - 1)),
            dma((chunks, ring - 1)),
            dma((chunks, per_chunk)),
            dma((chunks, per_chunk)),
            dma,
        ],
        compiler_params=pltpu.CompilerParams(
            collective_id=0, has_side_effects=True, vmem_limit_bytes=60 * 2**20
        ),
        name="finish",
    )(qkv, meta, meta.T, hidden, w_out)


def body(hidden, exit_depth, seq_ids, dest, norm_gain, w_query, w_key, w_value, w_out):
    peers = lax.axis_size("dp")
    groups = lax.axis_size("mp")
    meta = jnp.stack([seq_ids, jnp.where(exit_depth == 3, dest, -1)])
    qkv = project(hidden, norm_gain, w_query, w_key, w_value)
    return finish(qkv, meta, hidden, w_out, peers, groups)


def solution(mesh):
    return jax.shard_map(
        body,
        mesh=mesh,
        in_specs=(
            P("dp", None),
            P("dp"),
            P("dp"),
            P("dp"),
            P(),
            P(None, "mp"),
            P(None, "mp"),
            P(None, "mp"),
            P("mp", None),
        ),
        out_specs=P("dp", "mp"),
        check_vma=False,
    )
```

```python
import functools
import math

import jax
import jax.numpy as jnp
import numpy as np
from jax import lax
from jax.experimental import pallas as pl
from jax.experimental.pallas import tpu as pltpu
from jax.sharding import PartitionSpec as P

HD = 128
CHUNKS = 8
LAG = 1
ANY = pl.ANY
VMEM = pltpu.VMEM


def rope_tables(tokens):
    half = HD // 2
    frequency = 10000.0 ** (-np.arange(half, dtype=np.float64) / half)
    angle = np.arange(tokens, dtype=np.float64)[:, None] * frequency[None, :]
    cosine, sine = np.cos(angle), np.sin(angle)
    return (
        np.concatenate([cosine, cosine], axis=1).astype(np.float32),
        np.concatenate([-sine, sine], axis=1).astype(np.float32),
    )


def qkv_kernel(
    blocks, bn, rows, hidden, gain, wq, wk, wv, cosine, sine, out, held, normed, wbuf, hsem, wsem
):
    step = pl.program_id(0)
    slot = lax.rem(step, 2)
    chunks = hidden.shape[0] // rows

    def fetch(index, do):
        for which, w in enumerate((wq, wk, wv)):

            @pl.when(index // blocks == which)
            def _():
                column = pl.multiple_of(lax.rem(index, blocks) * bn, bn)
                to = lax.rem(index, 2)
                do(pltpu.make_async_copy(w.at[:, pl.ds(column, bn)], wbuf.at[to], wsem.at[to]))

    def hidden_copy(r):
        part = pl.ds(r * rows, rows)
        return pltpu.make_async_copy(hidden.at[part], held.at[part], hsem.at[r])

    @pl.when(step == 0)
    def _():
        for r in range(chunks):
            hidden_copy(r).start()
        fetch(0, lambda c: c.start())

    @pl.when(step + 1 < 3 * blocks)
    def _():
        fetch(step + 1, lambda c: c.start())

    @pl.when(step == 0)
    def _():
        def normalize(r, carry):
            hidden_copy(r).wait()
            part = pl.ds(pl.multiple_of(r * rows, rows), rows)
            x = held[part, :].astype(jnp.float32)
            mean_square = jnp.mean(x * x, axis=-1, keepdims=True)
            y = x * lax.rsqrt(mean_square + 1e-05) * gain[...].astype(jnp.float32)[None, :]
            normed[part, :] = y.astype(jnp.bfloat16)
            return carry

        lax.fori_loop(0, chunks, normalize, 0)

    fetch(step, lambda c: c.wait())
    big = 2 * rows

    def product(r, rotate):
        part = pl.ds(pl.multiple_of(r * big, big), big)
        y = jnp.dot(normed[part, :], wbuf[slot], preferred_element_type=jnp.float32)
        for h in range(bn // HD):
            lanes = slice(h * HD, (h + 1) * HD)
            z = y[:, lanes]
            if rotate:
                z = z * cosine[part, :] + pltpu.roll(z, HD // 2, 1) * sine[part, :]
            out[0, part, lanes] = z.astype(jnp.bfloat16)

    for rotate in (True, False):

        @pl.when((step < 2 * blocks) == rotate)
        def _():
            def go(r, carry):
                product(r, rotate)
                return carry

            lax.fori_loop(0, hidden.shape[0] // big, go, 0)


def project(hidden, gain, wq, wk, wv):
    tokens, width = hidden.shape
    hw = wq.shape[1]
    bn = 256 if hw % 256 == 0 else HD
    blocks = hw // bn
    rows = 128
    cosine, sine = rope_tables(tokens)
    whole = lambda *shape: pl.BlockSpec(shape, lambda i: (0,) * len(shape), pipeline_mode=pl.Buffered(1))
    return pl.pallas_call(
        functools.partial(qkv_kernel, blocks, bn, rows),
        grid=(3 * blocks,),
        out_shape=jax.ShapeDtypeStruct((3, tokens, hw), jnp.bfloat16),
        in_specs=[
            pl.BlockSpec(memory_space=ANY),
            whole(width),
            pl.BlockSpec(memory_space=ANY),
            pl.BlockSpec(memory_space=ANY),
            pl.BlockSpec(memory_space=ANY),
            whole(tokens, HD),
            whole(tokens, HD),
        ],
        out_specs=pl.BlockSpec((1, tokens, bn), lambda i: (i // blocks, 0, lax.rem(i, blocks))),
        scratch_shapes=[
            VMEM((tokens, width), jnp.bfloat16),
            VMEM((tokens, width), jnp.bfloat16),
            VMEM((2, width, bn), jnp.bfloat16),
            pltpu.SemaphoreType.DMA((tokens // rows,)),
            pltpu.SemaphoreType.DMA((2,)),
        ],
        compiler_params=pltpu.CompilerParams(vmem_limit_bytes=60 * 2**20),
        name="qkv",
    )(hidden, gain, wq, wk, wv, cosine, sine)


def tail_kernel(
    peers, groups, per_chunk, qkv, meta_row, hidden, w_out, out,
    wbuf, residual, slot_row, pair_send, pair_own, pair_recv, x_send, x_recv, acc, updated,
    wsem, rsem, pair_ssem, pair_rsem, x_ssem, x_rsem, row_ssem, row_rsem, own_sem,
):
    chunks, ring, rows, feature_slice = pair_send.shape
    capacity = rows // per_chunk
    _, tokens, inner = qkv.shape
    d, m = lax.axis_index("dp"), lax.axis_index("mp")
    core, x = lax.rem(m, 2), m // 2
    partner = x * 2 + 1 - core
    scale = 1.0 / math.sqrt(HD)
    mesh_id = pl.DeviceIdType.MESH

    def x_to(r):
        return lax.rem(x + r, ring)

    def target(i):
        away = peers // 2 + ((i + 1) // 2) * (1 - 2 * lax.rem(i, 2))
        return lax.rem(d + away, peers)

    def weight_copy(n):
        columns = pl.ds(n * feature_slice, feature_slice)
        return pltpu.make_async_copy(w_out.at[:, columns], wbuf.at[n], wsem.at[n])

    def residual_copy():
        columns = pl.ds(pl.multiple_of(m * feature_slice, HD), feature_slice)
        return pltpu.make_async_copy(hidden.at[:, columns], residual, rsem)

    def pair_copy(j):
        return pltpu.make_async_remote_copy(
            src_ref=pair_send.at[j], dst_ref=pair_recv.at[j],
            send_sem=pair_ssem.at[j], recv_sem=pair_rsem.at[j],
            device_id={"mp": partner}, device_id_type=mesh_id,
        )

    def x_copy(j, r):
        return pltpu.make_async_remote_copy(
            src_ref=x_send.at[j, r - 1], dst_ref=x_recv.at[j, r - 1],
            send_sem=x_ssem.at[j, r - 1], recv_sem=x_rsem.at[j, r - 1],
            device_id={"mp": x_to(r) * 2 + core}, device_id_type=mesh_id,
        )

    def own_rows():
        return out.at[pl.ds(pl.multiple_of(d * capacity, 16), capacity)]

    def row_copy(j, k):
        return pltpu.make_async_remote_copy(
            src_ref=updated.at[j, pl.ds(k * capacity, capacity)], dst_ref=own_rows(),
            send_sem=row_ssem.at[j, k], recv_sem=row_rsem.at[j, k],
            device_id={"dp": target(j * per_chunk + k)}, device_id_type=mesh_id,
        )

    def own_copy():
        return pltpu.make_async_copy(
            updated.at[chunks - 1, pl.ds(rows - capacity, capacity)], own_rows(), own_sem
        )

    for n in range(groups):
        weight_copy(n).start()
    residual_copy().start()

    barrier = pltpu.get_barrier_semaphore()
    for i in range(1, peers):
        pl.semaphore_signal(
            barrier, inc=1, device_id={"dp": lax.rem(d + i, peers)}, device_id_type=mesh_id
        )
    for r in range(1, ring):
        pl.semaphore_signal(
            barrier, inc=1, device_id={"mp": x_to(r) * 2 + core}, device_id_type=mesh_id
        )
    pl.semaphore_signal(barrier, inc=1, device_id={"mp": partner}, device_id_type=mesh_id)

    code = meta_row[1:2, :]
    hot_shape = (max(16, peers), tokens)
    hot = jnp.where(lax.broadcasted_iota(jnp.int32, hot_shape, 0) == code, 1.0, 0.0)
    below = lax.broadcasted_iota(jnp.int32, (tokens, tokens), 0)
    across = lax.broadcasted_iota(jnp.int32, (tokens, tokens), 1)
    before = jnp.where(below < across, 1.0, 0.0).astype(jnp.bfloat16)
    count = jnp.dot(hot.astype(jnp.bfloat16), before, preferred_element_type=jnp.float32)
    rank = jnp.sum(hot * count, axis=0, keepdims=True)
    slot_row[...] = jnp.where(code >= 0, code * capacity + rank.astype(jnp.int32), -1)

    pl.semaphore_wait(barrier, peers + ring - 1)
    def chosen(j):
        parts = []
        for k in range(per_chunk):
            row = lax.broadcasted_iota(jnp.int32, (capacity, tokens), 0)
            parts.append((row + target(j * per_chunk + k) * capacity) == slot_row[...])
        return jnp.concatenate(parts, axis=0) if per_chunk > 1 else parts[0]

    def as_pick(hit):
        return jnp.where(hit, 1.0, 0.0).astype(jnp.bfloat16)

    def attend(j):
        hit = chosen(j)
        places = lax.broadcasted_iota(jnp.int32, (rows, tokens), 1)
        weight = jnp.where(hit, 1.0, 0.0)
        filled = jnp.sum(weight, axis=-1, keepdims=True)
        place = jnp.sum(jnp.where(hit, places, 0).astype(jnp.float32), axis=-1, keepdims=True)
        documents = meta_row[0:1, :].astype(jnp.float32)
        document = jnp.sum(jnp.where(hit, documents, 0.0), axis=-1, keepdims=True)
        allowed = (document == documents) & (places.astype(jnp.float32) <= place)
        bias = jnp.where(allowed, 0.0, -1e30)
        queries = jnp.dot(
            weight.astype(jnp.bfloat16), qkv[0], preferred_element_type=jnp.float32
        ).astype(jnp.bfloat16)
        heads = []
        for h in range(inner // HD):
            lanes = slice(h * HD, (h + 1) * HD)
            scores = lax.dot_general(
                queries[:, lanes], qkv[1, :, lanes], (((1,), (1,)), ((), ())),
                preferred_element_type=jnp.float32,
            )
            scores = scores * scale + bias
            raised = jnp.exp(scores - jnp.max(scores, axis=-1, keepdims=True))
            total = jnp.sum(raised, axis=-1, keepdims=True)
            mixed = jnp.dot(
                raised.astype(jnp.bfloat16), qkv[2, :, lanes], preferred_element_type=jnp.float32
            )
            heads.append((mixed * (filled / total)).astype(jnp.bfloat16))
        return jnp.concatenate(heads, axis=1)

    def multiply(attended, n):
        return jnp.dot(attended, wbuf[n], preferred_element_type=jnp.float32).astype(jnp.bfloat16)

    def step(s, carry):
        @pl.when(s < chunks)
        def _():
            attended = attend(s)

            @pl.when(s == 0)
            def _():
                for n in range(groups):
                    weight_copy(n).wait()
                residual_copy().wait()

            for r in range(ring):
                pair_send[s, r] = multiply(attended, x_to(r) * 2 + 1 - core)
            pair_copy(s).start()
            for r in range(ring):
                pair_own[s, r] = multiply(attended, x_to(r) * 2 + core)
            pair_copy(s).wait_recv()
            for r in range(1, ring):
                total = pair_own[s, r].astype(jnp.float32) + pair_recv[s, r].astype(jnp.float32)
                x_send[s, r - 1] = total.astype(jnp.bfloat16)
                x_copy(s, r).start()
            kept = jnp.dot(as_pick(chosen(s)), residual[...], preferred_element_type=jnp.float32)
            acc[s] = (
                kept + pair_own[s, 0].astype(jnp.float32) + pair_recv[s, 0].astype(jnp.float32)
            )

        @pl.when(s >= LAG)
        def _():
            j = s - LAG
            total = acc[j]
            for r in range(1, ring):
                x_copy(j, r).wait_recv()
                total += x_recv[j, r - 1].astype(jnp.float32)
            updated[j] = total.astype(jnp.bfloat16)
            for k in range(per_chunk - 1):
                row_copy(j, k).start()

            @pl.when(j < chunks - 1)
            def _():
                row_copy(j, per_chunk - 1).start()

        return carry

    lax.fori_loop(0, chunks + LAG, step, 0)
    own_copy().start()

    def drain(j, carry):
        pair_copy(j).wait_send()
        for r in range(1, ring):
            x_copy(j, r).wait_send()
        for k in range(per_chunk - 1):
            row_copy(j, k).wait()

        @pl.when(j < chunks - 1)
        def _():
            row_copy(j, per_chunk - 1).wait()

        return carry

    lax.fori_loop(0, chunks, drain, 0)
    own_copy().wait()


def finish(qkv, meta, hidden, w_out, peers, groups):
    _, tokens, inner = qkv.shape
    slots = 3 * tokens // 4
    feature_slice = w_out.shape[1] // groups
    chunks = min(CHUNKS, peers)
    rows = slots // chunks
    ring = groups // 2
    dma = pltpu.SemaphoreType.DMA
    bf16 = jnp.bfloat16
    vmem = pl.BlockSpec(memory_space=VMEM)
    far = pl.BlockSpec(memory_space=ANY)
    per_chunk = peers // chunks
    return pl.pallas_call(
        functools.partial(tail_kernel, peers, groups, per_chunk),
        out_shape=jax.ShapeDtypeStruct((slots, feature_slice), bf16),
        in_specs=[vmem, vmem, far, far],
        out_specs=far,
        scratch_shapes=[
            VMEM((groups, inner, feature_slice), bf16),
            VMEM((tokens, feature_slice), bf16),
            VMEM((1, tokens), jnp.int32),
            VMEM((chunks, ring, rows, feature_slice), bf16),
            VMEM((chunks, ring, rows, feature_slice), bf16),
            VMEM((chunks, ring, rows, feature_slice), bf16),
            VMEM((chunks, ring - 1, rows, feature_slice), bf16),
            VMEM((chunks, ring - 1, rows, feature_slice), bf16),
            VMEM((chunks, rows, feature_slice), jnp.float32),
            VMEM((chunks, rows, feature_slice), bf16),
            dma((groups,)),
            dma,
            dma((chunks,)),
            dma((chunks,)),
            dma((chunks, ring - 1)),
            dma((chunks, ring - 1)),
            dma((chunks, per_chunk)),
            dma((chunks, per_chunk)),
            dma,
        ],
        compiler_params=pltpu.CompilerParams(
            collective_id=0, has_side_effects=True, vmem_limit_bytes=60 * 2**20
        ),
        name="finish",
    )(qkv, meta, hidden, w_out)


def body(hidden, exit_depth, seq_ids, dest, norm_gain, w_query, w_key, w_value, w_out):
    peers = lax.axis_size("dp")
    groups = lax.axis_size("mp")
    meta = jnp.stack([seq_ids, jnp.where(exit_depth == 3, dest, -1)])
    qkv = project(hidden, norm_gain, w_query, w_key, w_value)
    return finish(qkv, meta, hidden, w_out, peers, groups)


def solution(mesh):
    return jax.shard_map(
        body,
        mesh=mesh,
        in_specs=(
            P("dp", None),
            P("dp"),
            P("dp"),
            P("dp"),
            P(),
            P(None, "mp"),
            P(None, "mp"),
            P(None, "mp"),
            P("mp", None),
        ),
        out_specs=P("dp", "mp"),
        check_vma=False,
    )
```
